32 devices in a mesh: wide: 16 (over z, x, core), ctr: 2 (over y).
Axes of the slice: x: 2, y: 2, z: 4, core: 2. Of those that a mesh axis runs over, the one named last changes fastest.
Arguments:
- tens: bfloat16 [2048, 256, 128], P(('wide', 'ctr')), may hold values from -0.29882812 to 0.29882812
- coef: bfloat16 [120, 2048], P(None, 'wide'), may hold values from -0.5 to 0.5
- aux_of: int32 [2048, 1], P(('wide', 'ctr')), may hold values from 0 to 15; in each aligned block of 64 rows (0 to 63, 64 to 127, ...) at most 8 rows name the same one
- slot_of: int32 [2048], P(('wide', 'ctr')), may hold values from 0 to 7
- metric: bfloat16 [16, 256, 256], P('wide'), as said below
Outputs:
- exchange: float32 [120, 2048], P(None, ('wide', 'ctr'))
The draws below stay inside these ranges and needn't reach their ends.
Inputs may be any that keep to these rules, and one draw needn't show every extreme that they name: `aux_of`: among the blocks of one device at most 8 name the same auxiliary block, and in every draw some device has exactly 8 that do. `metric`: each block is symmetric.
All inputs are finite; a program needn't handle non-finite values.
Results may differ from the reference program's by a relative error of at most 0.0011.
Values may be sent and summed in bfloat16 or wider, within the bound.
No kernel may reach another device: no remote copies, remote signals or barrier semaphores. Data moves between devices by JAX's collectives and lax.ppermute only.
A program may use at most 64 MiB of HBM per device.

```python
import math
import jax
import jax.numpy as jnp
import numpy as np
from jax import lax

AB = 256
OB = 128
NJ = 120
BLK_DEV = 64
OCC_DEV = 8
CAP = 8
NBLK = 2048
NMU = 2048
NAUXB = 16
N_WIDE = 16
N_CTR = 2


def draw_metric(key, part):
    raw = jax.random.normal(jax.random.fold_in(key, 11), (NAUXB, AB, AB), jnp.float32)
    sym = (raw + jnp.swapaxes(raw, 1, 2)) * (0.6 / math.sqrt(2.0 * AB))
    diag_scale = jax.random.uniform(jax.random.fold_in(key, 12), (NAUXB, 1, AB), jnp.float32, 0.5, 2.0)
    identity = jnp.eye(AB, dtype=jnp.float32)[None, :, :]
    return (sym + identity * (1.0 + diag_scale)).astype(jnp.bfloat16)


def plant(values, key, low, top_value):
    longest = values.shape.index(max(values.shape))
    spots = []
    for shift in (0, 1):
        where = [jax.random.randint(jax.random.fold_in(key, axis), (), 0, length) for axis, length in enumerate(values.shape)]
        where[longest] = (where[longest] + shift) % values.shape[longest]
        spots.append(tuple(where))
    return values.at[spots[0]].set(low).at[spots[1]].set(top_value)


def steps_of(rng, dims, split, least, high):
    level, own = 1.0, jax.random.fold_in(rng, 6)
    for axis_at, parts in split:
        heights = jnp.exp(jax.random.uniform(jax.random.fold_in(own, axis_at), (parts,), jnp.float32, least / len(split), high / len(split)))
        level = level * jnp.repeat(heights, dims[axis_at] // parts).reshape([-1 if axis == axis_at else 1 for axis in range(len(dims))])
    return level


def routed_block(rng, own, number, rows, amount, top, bound, lean):
    order = jax.random.permutation(rng, amount)
    heavy_load, common = shares(amount, rows * top, bound, lean, True), shares(amount, rows * top, bound, lean, False)
    places = jnp.arange(amount)

    def named(sizes, turn):
        used = int((sizes > 0).sum())
        fixed = max(1, used // 4)
        passed = fixed + (places - fixed + turn * (used - fixed)) % max(1, amount - fixed)
        return jnp.zeros((amount,), jnp.int32).at[order[jnp.where(places < fixed, places, passed)]].set(jnp.asarray(sizes, jnp.int32))

    sizes = jnp.where(number % 4 == 0, named(heavy_load, number // 4), named(common, number - number // 4 - 1))
    mixed = jax.random.permutation(jax.random.fold_in(own, 3), amount)
    donor, receiver = mixed[0:amount // 2 * 2:2], mixed[1:amount // 2 * 2:2]
    room = jnp.minimum(sizes[donor] - 1, bound - sizes[receiver]) // 2
    room = jnp.where((donor == order[0]) | (receiver == order[0]) | (sizes[receiver] == 0), 0, jnp.maximum(room, 0))
    passed = jax.random.randint(jax.random.fold_in(own, 4), (amount // 2,), 0, 1 << 20) % (room + 1)
    sizes = sizes.at[donor].add(-passed).at[receiver].add(passed)
    members = jnp.searchsorted(jnp.cumsum(sizes), jnp.arange(rows * top), side="right").astype(jnp.int32)
    listing = members.reshape(top, rows).T
    listing = listing[jax.random.permutation(jax.random.fold_in(own, 1), rows)]
    turn = jax.random.randint(jax.random.fold_in(own, 2), (rows, 1), 0, top)
    return jnp.take_along_axis(listing, (jnp.arange(top)[None, :] + turn) % top, axis=1)


def shares(count, total, most, skew, full):
    weights = [(1 << 20) // math.isqrt(rank ** skew) + 1 for rank in range(1, count + 1)]
    largest = most if full else min(most, max(-(-total // count), total * weights[0] // sum(weights)))
    least = 1 if total - largest >= count - 1 else 0
    counts, surplus = [largest] + [least] * (count - 1), total - largest - least * (count - 1)
    while surplus > 0:
        candidates = [i for i in range(1, count) if counts[i] < largest] or [i for i in range(1, count) if counts[i] < most]
        mass, left = sum([weights[i] for i in candidates]), surplus
        for i in candidates:
            more = min(most - counts[i], max(1, left * weights[i] // mass), surplus)
            counts[i] = counts[i] + more
            surplus = surplus - more
    return np.array(counts)


def noise(rng, shape, spread, limit, split=(), kind=jnp.bfloat16):
    values = spread * jax.random.normal(rng, shape, jnp.float32)
    if split:
        values = values * steps_of(rng, shape, split, -0.22, 0.18)
    return jnp.clip(values, -limit, limit).astype(kind)


def setup_inputs(seed: int = 0) -> dict:
    streams_of = jax.random.split(jax.random.key(seed), 6)
    tens = noise(streams_of[0], (NBLK, AB, OB), 0.05, 0.29882812, ((0, 32),))
    coef = noise(streams_of[1], (NJ, NMU), OB ** -0.5, 0.5, ((1, 16),))
    aux_of_keys = jax.random.split(jax.random.fold_in(streams_of[2], 1), NBLK // BLK_DEV)
    aux_of_turns = jax.random.permutation(jax.random.fold_in(streams_of[2], 3), NBLK // BLK_DEV)
    aux_of = jax.vmap(lambda own, number: routed_block(jax.random.fold_in(streams_of[2], 2), own, number, BLK_DEV, N_WIDE, 1, CAP, 2))(aux_of_keys, aux_of_turns).reshape((NBLK, 1))
    slot_of = plant(jax.random.randint(streams_of[3], (NBLK,), 0, OCC_DEV), jax.random.fold_in(streams_of[3], 1), 0, OCC_DEV - 1).astype(jnp.int32)
    metric = draw_metric(jax.random.fold_in(streams_of[5], 71), 0)
    return {"tens": tens, "coef": coef, "aux_of": aux_of, "slot_of": slot_of, "metric": metric}


def reference(tens, coef, aux_of, slot_of, metric):
    owners = N_WIDE
    groups = N_CTR
    blocks = tens.reshape(owners, groups, BLK_DEV, AB, OB)
    targets = aux_of.reshape(owners, groups, BLK_DEV)
    slot_ids = slot_of.reshape(owners, groups, BLK_DEV)
    columns = coef.reshape(NJ, owners, OB).astype(jnp.float32)
    metric_full = metric.astype(jnp.float32)

    def per_group(result, group_id):
        def add_owner(fitted, owner_id):
            local_rows = blocks[owner_id, group_id].astype(jnp.float32)
            half_form = jnp.einsum("jm,bpm->bjp", columns[:, owner_id], local_rows).astype(jnp.bfloat16)
            half_form = lax.optimization_barrier(half_form).astype(jnp.float32)
            positions = (targets[owner_id, group_id] * OCC_DEV + slot_ids[owner_id, group_id]).astype(jnp.int32)
            return fitted.at[positions].add(half_form), None

        fitted, unused = lax.scan(add_owner, jnp.zeros((owners * OCC_DEV, NJ, AB), jnp.float32), jnp.arange(owners))
        rounded = lax.optimization_barrier(fitted.astype(jnp.bfloat16)).astype(jnp.float32)
        rounded = rounded.reshape(owners, OCC_DEV, NJ, AB)
        weighted = jnp.einsum("asjp,apq->asjq", rounded, metric_full).astype(jnp.bfloat16)
        weighted = lax.optimization_barrier(weighted).astype(jnp.float32).reshape(owners * OCC_DEV, NJ, AB)

        def add_back(totals, owner_id):
            positions = (targets[owner_id, group_id] * OCC_DEV + slot_ids[owner_id, group_id]).astype(jnp.int32)
            local_rows = blocks[owner_id, group_id].astype(jnp.float32)
            contribution = jnp.einsum("bjq,bqm->jm", weighted[positions], local_rows)
            return totals.at[:, owner_id].add(contribution), None

        result, unused = lax.scan(add_back, result, jnp.arange(owners))
        return result, None

    result, unused = lax.scan(per_group, jnp.zeros((NJ, owners, OB), jnp.float32), jnp.arange(groups))
    return result.reshape(NJ, owners * OB)
```

```python
import functools

import jax
import jax.numpy as jnp
from jax import lax
from jax.experimental import pallas as pl
from jax.experimental.pallas import tpu as pltpu
from jax.sharding import PartitionSpec as P

OCC_DEV = 8
GROUP = 4
MIB = 1 << 20


def ring_place(chip, chips):
    return jnp.where(chip % 2 == 0, chip // 2, chips - 1 - chip // 2)


def ring_pairs(chips, step):
    order = list(range(0, chips, 2)) + list(range(1, chips, 2))[::-1]
    return [
        (2 * order[k] + core, 2 * order[(k + step) % chips] + core)
        for k in range(chips)
        for core in range(2)
    ]


def sum_cells_kernel(order, cell, tens, coef, out, total):
    out[...] = jnp.zeros_like(out)
    block_count = tens.shape[0]

    def group(g, carry):
        halves, cells, firsts = [], [], []
        for u in range(GROUP):
            k = g * GROUP + u
            b = order[k]
            here = cell[b]
            before = cell[order[jnp.maximum(k - 1, 0)]]
            half = lax.dot_general(
                coef[...], tens[b], (((1,), (1,)), ((), ())), preferred_element_type=jnp.float32
            )
            halves.append(half.astype(jnp.bfloat16).astype(jnp.float32))
            cells.append(here)
            firsts.append(jnp.logical_or(k == 0, before != here))
        for half, here, first in zip(halves, cells, firsts):
            keep = jnp.where(first, 0.0, 1.0)
            value = total[...] * keep + half
            total[...] = value
            out[here] = value.astype(jnp.bfloat16)
        return carry

    total[...] = jnp.zeros_like(total)
    lax.fori_loop(0, block_count // GROUP, group, 0)


def sum_cells(order, cell, tens, coef, cells):
    rows, width = coef.shape[0], tens.shape[1]
    return pl.pallas_call(
        sum_cells_kernel,
        out_shape=jax.ShapeDtypeStruct((cells, rows, width), jnp.bfloat16),
        grid_spec=pltpu.PrefetchScalarGridSpec(
            num_scalar_prefetch=2,
            grid=(1,),
            in_specs=[
                pl.BlockSpec(tens.shape, lambda i, *_: (0, 0, 0), pipeline_mode=pl.Buffered(1)),
                pl.BlockSpec(coef.shape, lambda i, *_: (0, 0), pipeline_mode=pl.Buffered(1)),
            ],
            out_specs=pl.BlockSpec(
                (cells, rows, width), lambda i, *_: (0, 0, 0), pipeline_mode=pl.Buffered(1)
            ),
            scratch_shapes=[pltpu.VMEM((rows, width), jnp.float32)],
        ),
        compiler_params=pltpu.CompilerParams(vmem_limit_bytes=24 * MIB),
        name="sum_cells",
    )(order, cell, tens, coef)


def apply_cells_kernel(cell, weighted, tens, out):
    block_count = tens.shape[0]

    def group(g, total):
        for u in range(GROUP):
            b = g * GROUP + u
            total = total + jnp.dot(
                weighted[cell[b]], tens[b], preferred_element_type=jnp.float32
            )
        return total

    out[...] = lax.fori_loop(0, block_count // GROUP, group, jnp.zeros(out.shape, jnp.float32))


def apply_cells(cell, weighted, tens):
    rows, width = weighted.shape[1], tens.shape[2]
    return pl.pallas_call(
        apply_cells_kernel,
        out_shape=jax.ShapeDtypeStruct((rows, width), jnp.float32),
        grid_spec=pltpu.PrefetchScalarGridSpec(
            num_scalar_prefetch=1,
            grid=(1,),
            in_specs=[
                pl.BlockSpec(weighted.shape, lambda i, *_: (0, 0, 0), pipeline_mode=pl.Buffered(1)),
                pl.BlockSpec(tens.shape, lambda i, *_: (0, 0, 0), pipeline_mode=pl.Buffered(1)),
            ],
            out_specs=pl.BlockSpec((rows, width), lambda i, *_: (0, 0)),
        ),
        compiler_params=pltpu.CompilerParams(vmem_limit_bytes=24 * MIB),
        name="apply_cells",
    )(cell, weighted, tens)


def sum_over_ctr(partial_value):
    if lax.axis_size("ctr") != 2:
        return lax.psum_scatter(partial_value, "ctr", scatter_dimension=1, tiled=True)
    width = partial_value.shape[1] // 2
    low, high = partial_value[:, :width], partial_value[:, width:]
    first = lax.axis_index("ctr") == 0
    mine, other = jnp.where(first, low, high), jnp.where(first, high, low)
    return mine + lax.ppermute(other, "ctr", [(0, 1), (1, 0)])


def cells_body(tens, coef, aux_of, slot_of, metric):
    owners = lax.axis_size("wide")
    chips = owners // 2
    far = chips // 2
    slots = OCC_DEV
    block_count = tens.shape[0]
    me = lax.axis_index("wide")
    core, place = me % 2, ring_place(me // 2, chips)
    forward = functools.partial(lax.ppermute, axis_name="wide", perm=ring_pairs(chips, 1))
    backward = functools.partial(lax.ppermute, axis_name="wide", perm=ring_pairs(chips, -1))
    across = functools.partial(
        lax.ppermute, axis_name="wide", perm=[(k, k ^ 1) for k in range(owners)]
    )

    target = aux_of[:, 0]
    ahead = (ring_place(target // 2, chips) - place) % chips
    other_core = jnp.where(target % 2 == core, 0, 1)
    cell = (other_core * chips + ahead) * slots + slot_of
    series = jnp.arange(block_count)
    key = cell * block_count + series
    rank = jnp.sum(jnp.where(key[None, :] < key[:, None], 1, 0), axis=1)
    order = jnp.sum(jnp.where(rank[None, :] == series[:, None], series[None, :], 0), axis=1)

    sums = sum_cells(order, cell, tens, coef, 2 * chips * slots)
    halves = [slice(0, slots // 2), slice(slots // 2, slots)]

    def at(kind, ahead):
        start = (kind * chips + ahead) * slots
        return sums[start : start + slots]

    local = {}
    for step in range(far, -1, -1):
        for r in sorted({step, (chips - step) % chips}):
            got = across(at(1, r))
            local[r] = [
                at(0, r)[h].astype(jnp.float32) + got[h].astype(jnp.float32) for h in halves
            ]

    def add(value, held):
        return held if value is None else value.astype(jnp.float32) + held

    up, down = [None, None], [None, None]
    for step in range(far, 0, -1):
        for h in range(2):
            if step < far or h == 0:
                up[h] = forward(add(up[h], local[step][h]).astype(jnp.bfloat16))
            if step < far or h == 1:
                down[h] = backward(add(down[h], local[chips - step][h]).astype(jnp.bfloat16))

    own = []
    for h in range(2):
        fitted = add(down[h], add(up[h], local[0][h])).astype(jnp.bfloat16)
        own.append(
            jnp.einsum(
                "sjp,pq->sjq", fitted, metric[0], preferred_element_type=jnp.float32
            ).astype(jnp.bfloat16)
        )

    held = {0: list(own)}
    up, down = list(own), list(own)
    for step in range(1, far + 1):
        for r in (chips - step, step):
            held.setdefault(r, [None, None])
        for h in range(2):
            if step < far or h == 0:
                up[h] = forward(up[h])
                held[chips - step][h] = up[h]
            if step < far or h == 1:
                down[h] = backward(down[h])
                held[step][h] = down[h]

    pieces = [jnp.concatenate(held[r]) for r in range(chips)]
    others = [across(piece) for piece in pieces]
    partial_value = apply_cells(cell, jnp.concatenate(pieces + others), tens)
    return sum_over_ctr(partial_value)


def slots_body(tens, coef, aux_of, slot_of, metric):
    owners = lax.axis_size("wide")
    block_count = tens.shape[0]
    capacity = max(2, 2 * block_count // owners)
    total_slots = owners * capacity
    half_form = jnp.einsum("jm,bpm->bjp", coef, tens, preferred_element_type=jnp.float32).astype(
        jnp.bfloat16
    )
    target = aux_of[:, 0]
    series = jnp.arange(block_count)
    matches = target[:, None] == target[None, :]
    earlier = series[None, :] < series[:, None]
    ranking = jnp.sum(jnp.where(matches & earlier, 1, 0), axis=1)
    position = target * capacity + ranking
    selector = position[None, :] == jnp.arange(total_slots)[:, None]
    selector_bf = jnp.where(selector, 1.0, 0.0).astype(jnp.bfloat16)
    outgoing = jnp.einsum(
        "kb,bjp->kjp", selector_bf, half_form, preferred_element_type=jnp.float32
    ).astype(jnp.bfloat16)
    slot_tags = jnp.sum(jnp.where(selector, slot_of[None, :] + 1, 0), axis=1)
    received, tags_in = (
        lax.all_to_all(outgoing, "wide", split_axis=0, concat_axis=0, tiled=True),
        lax.all_to_all(slot_tags, "wide", split_axis=0, concat_axis=0, tiled=True),
    )
    slot_onehot = jnp.where(
        tags_in[None, :] == (jnp.arange(OCC_DEV) + 1)[:, None], 1.0, 0.0
    ).astype(jnp.bfloat16)
    fitted = jnp.einsum(
        "sk,kjp->sjp", slot_onehot, received, preferred_element_type=jnp.float32
    ).astype(jnp.bfloat16)
    weighted = jnp.einsum(
        "sjp,pq->sjq", fitted, metric[0], preferred_element_type=jnp.float32
    ).astype(jnp.bfloat16)
    answers = jnp.einsum(
        "sk,sjq->kjq", slot_onehot, weighted, preferred_element_type=jnp.float32
    ).astype(jnp.bfloat16)
    returned = lax.all_to_all(answers, "wide", split_axis=0, concat_axis=0, tiled=True)
    per_block = jnp.einsum(
        "kb,kjq->bjq", selector_bf, returned, preferred_element_type=jnp.float32
    ).astype(jnp.bfloat16)
    partial_value = jnp.einsum("bjq,bqm->jm", per_block, tens, preferred_element_type=jnp.float32)
    return sum_over_ctr(partial_value)


def body(tens, coef, aux_of, slot_of, metric):
    owners, block_count = lax.axis_size("wide"), tens.shape[0]
    dense = owners * OCC_DEV <= 2 * block_count and owners % 4 == 0
    return (cells_body if dense else slots_body)(tens, coef, aux_of, slot_of, metric)


def solution(mesh):
    placed = (
        P(("wide", "ctr"), None, None),
        P(None, "wide"),
        P(("wide", "ctr"), None),
        P(("wide", "ctr")),
        P("wide", None, None),
    )
    return jax.shard_map(
        body, mesh=mesh, in_specs=placed, out_specs=P(None, ("wide", "ctr")), check_vma=False
    )
```

```python
import functools

import jax
import jax.numpy as jnp
from jax import lax
from jax.experimental import pallas as pl
from jax.experimental.pallas import tpu as pltpu
from jax.sharding import PartitionSpec as P

OCC_DEV = 8
GROUP = 4
CHUNKS = 8
KERNEL_VMEM = 28 << 20


def ring_place(chip, chips):
    return jnp.where(chip % 2 == 0, chip // 2, chips - 1 - chip // 2)


def ring_pairs(chips, step):
    order = list(range(0, chips, 2)) + list(range(1, chips, 2))[::-1]
    return [
        (2 * order[k] + core, 2 * order[(k + (step, -step)[core]) % chips] + core)
        for k in range(chips)
        for core in range(2)
    ]


def whole(x):
    return pl.BlockSpec(x.shape, lambda i, *_: (0,) * len(x.shape), pipeline_mode=pl.Buffered(1))


def cost(blocks, tens, rows, more):
    width, depth = tens.shape[1:]
    return pl.CostEstimate(
        flops=2 * blocks * rows * width * depth,
        bytes_accessed=2 * blocks * width * depth + more,
        transcendentals=0,
    )


def sum_cells_kernel(sends, cell, again, tens, coef, *refs):
    out, copied, (blocks, rows_in, totals, arrived) = refs[0], refs[1:-4], refs[-4:]
    block_count = tens.shape[0]
    chunk = block_count // CHUNKS
    copies = [pltpu.make_async_copy(coef, rows_in, arrived.at[CHUNKS])]
    for c in range(CHUNKS):
        part = slice(c * chunk, (c + 1) * chunk)
        copies.append(pltpu.make_async_copy(tens.at[part], blocks.at[part], arrived.at[c]))
    for copy in copies:
        copy.start()
    out[...] = jnp.zeros_like(out)
    copies[0].wait()
    for c in range(CHUNKS):
        copies[1 + c].wait()
        for start in range(c * chunk, (c + 1) * chunk, GROUP):
            halves = [
                lax.dot_general(
                    rows_in[...],
                    blocks[b],
                    (((1,), (1,)), ((), ())),
                    preferred_element_type=jnp.float32,
                )
                for b in range(start, start + GROUP)
            ]
            for b, half in zip(range(start, start + GROUP), halves):
                here = cell[b]
                half = half.astype(jnp.bfloat16).astype(jnp.float32)
                total = jnp.where(again[b] != 0, totals[here] + half, half)
                totals[here] = total
                out[here] = total.astype(jnp.bfloat16)
    for send, copy in zip(sends, copied):
        for k, c in enumerate(send):
            copy[k] = out[c]


def sum_cells(cell, again, tens, coef, cells, sends):
    rows, width = coef.shape[0], tens.shape[1]
    outs = [jax.ShapeDtypeStruct((cells, rows, width), jnp.bfloat16)]
    outs += [jax.ShapeDtypeStruct((len(send), rows, width), jnp.bfloat16) for send in sends]
    hbm = pl.BlockSpec(memory_space=pltpu.HBM)
    return pl.pallas_call(
        functools.partial(sum_cells_kernel, sends),
        out_shape=tuple(outs),
        grid_spec=pltpu.PrefetchScalarGridSpec(
            num_scalar_prefetch=2,
            grid=(1,),
            in_specs=[hbm, hbm],
            out_specs=tuple(whole(out) for out in outs),
            scratch_shapes=[
                pltpu.VMEM(tens.shape, tens.dtype),
                pltpu.VMEM(coef.shape, coef.dtype),
                pltpu.VMEM((cells, rows, width), jnp.float32),
                pltpu.SemaphoreType.DMA((CHUNKS + 1,)),
            ],
        ),
        compiler_params=pltpu.CompilerParams(vmem_limit_bytes=KERNEL_VMEM),
        cost_estimate=cost(tens.shape[0], tens, rows, 2 * cells * rows * width),
        name="sum_cells",
    )(
        cell,
        again,
        pltpu.with_memory_space_constraint(tens, pltpu.HBM),
        pltpu.with_memory_space_constraint(coef, pltpu.HBM),
    )


def apply_cells_kernel(step, sorted_blocks, bounds, order, cell, before, tens, *refs):
    count, first, low, high = step
    pieces, outs, held = refs[:count], refs[count:-1], refs[-1]
    slots = pieces[0].shape[0]
    for p, piece in enumerate(pieces):
        held[p * slots : (p + 1) * slots] = piece[...]
    empty = count * slots
    held[empty] = jnp.zeros(held.shape[1:], held.dtype)
    start, stop, last = bounds[low], bounds[high], order.shape[0] - 1

    def group(g, total):
        for u in range(GROUP):
            k = start + g * GROUP + u
            b = order[jnp.minimum(k, last)]
            here = jnp.where(k < stop, cell[b] - first, empty)
            at = jnp.minimum(k, tens.shape[0] - 1) if sorted_blocks else b
            total = total + jnp.dot(held[here], tens[at], preferred_element_type=jnp.float32)
        return total

    outs[0][...] = lax.fori_loop(0, (stop - start + GROUP - 1) // GROUP, group, before[...])
    if len(outs) > 1:
        for k in range(outs[1].shape[0]):
            outs[1][k] = tens[order[k]]


def apply_cells(step, bounds, order, cell, before, tens, pieces, most, sorted_blocks=False, take=0):
    rows, width = pieces[0].shape[1:]
    cells = len(pieces) * pieces[0].shape[0]
    outs = [jax.ShapeDtypeStruct(before.shape, jnp.float32)]
    if take:
        outs.append(jax.ShapeDtypeStruct((take, *tens.shape[1:]), tens.dtype))
    return pl.pallas_call(
        functools.partial(apply_cells_kernel, (len(pieces), *step), sorted_blocks),
        out_shape=tuple(outs),
        grid_spec=pltpu.PrefetchScalarGridSpec(
            num_scalar_prefetch=3,
            grid=(1,),
            in_specs=[whole(before), whole(tens)] + [whole(piece) for piece in pieces],
            out_specs=tuple(whole(out) for out in outs),
            scratch_shapes=[pltpu.VMEM((cells + 1, rows, width), jnp.bfloat16)],
        ),
        compiler_params=pltpu.CompilerParams(vmem_limit_bytes=KERNEL_VMEM),
        cost_estimate=cost(min(most, tens.shape[0]), tens, rows, 2 * cells * rows * width),
        name="apply_cells",
    )(bounds, order, cell, before, tens, *pieces)


def sum_over_ctr(partial_value):
    if lax.axis_size("ctr") != 2:
        return lax.psum_scatter(partial_value, "ctr", scatter_dimension=1, tiled=True)
    width = partial_value.shape[1] // 2
    low, high = partial_value[:, :width], partial_value[:, width:]
    first = lax.axis_index("ctr") == 0
    mine, other = jnp.where(first, low, high), jnp.where(first, high, low)
    return mine + lax.ppermute(other, "ctr", [(0, 1), (1, 0)])


def cells_body(tens, coef, aux_of, slot_of, metric):
    owners = lax.axis_size("wide")
    chips = owners // 2
    far = chips // 2
    slots = OCC_DEV
    block_count = tens.shape[0]
    me = lax.axis_index("wide")
    core, place = me % 2, ring_place(me // 2, chips)
    forward = functools.partial(lax.ppermute, axis_name="wide", perm=ring_pairs(chips, 1))
    backward = functools.partial(lax.ppermute, axis_name="wide", perm=ring_pairs(chips, -1))
    across = functools.partial(
        lax.ppermute, axis_name="wide", perm=[(k, k ^ 1) for k in range(owners)]
    )

    half_slots = slots // 2
    pieces_of, group_starts = {}, []
    for step in range(far, -1, -1):
        for h in range(2):
            group_starts.append(len(pieces_of))
            for r in sorted({step, (chips - step) % chips}):
                for kind in range(2):
                    pieces_of[r, h, kind] = len(pieces_of)
    group_starts.append(len(pieces_of))
    cells = len(pieces_of) * half_slots

    target = aux_of[:, 0]
    ahead = ring_place(target // 2, chips) - place
    ahead = jnp.where(target % 2 == 0, ahead, -ahead) % chips
    step_of = jnp.minimum(ahead, chips - ahead)
    paired = jnp.where((step_of == 0) | (step_of == far), 0, 1)
    piece = jnp.where(step_of == far, 0, 4 + (far - 1 - step_of) * 8)
    piece += (slot_of // half_slots) * (2 + 2 * paired) + 2 * paired * jnp.where(ahead > far, 1, 0)
    piece += jnp.where(target % 2 == core, 0, 1)
    cell = piece * half_slots + slot_of % half_slots
    series = jnp.arange(block_count)
    key = cell * block_count + series
    rank = jnp.sum(jnp.where(key[None, :] < key[:, None], 1, 0), axis=1)
    order = jnp.sum(jnp.where(rank[None, :] == series[:, None], series[None, :], 0), axis=1)
    limits = jnp.array([start * half_slots for start in group_starts], jnp.int32)
    bounds = jnp.sum(jnp.where(cell[None, :] < limits[:, None], 1, 0), axis=1)

    apart = lax.optimization_barrier
    capacity = 2 * block_count // owners
    same = (cell[None, :] == cell[:, None]) & (series[None, :] < series[:, None])
    again = jnp.sum(jnp.where(same, 1, 0), axis=1)
    sent = [(r, h) for r, h, kind in pieces_of if kind == 1]
    sends = [[], []]
    for r, h in sent:
        start = pieces_of[r, h, 1] * half_slots
        sends[r != far] += range(start, start + half_slots)
    sums, *others = sum_cells(cell, again, tens, coef, cells, sends)
    got = [across(others[0])]
    got[0], others[1] = apart((got[0], others[1]))
    got.append(across(others[1]))
    local = {}
    for k, (r, h) in enumerate(sent):
        start = pieces_of[r, h, 0] * half_slots
        mine = apart(sums[start : start + half_slots])
        start = (k if r == far else k - 2) * half_slots
        other = apart(got[r != far][start : start + half_slots])
        local[r, h] = mine.astype(jnp.float32) + other.astype(jnp.float32)

    def add(value, held):
        return held if value is None else apart(value).astype(jnp.float32) + held

    up, down = [None, None], [None, None]
    for step in range(far, 0, -1):
        for h in range(2):
            if step < far or h == 0:
                up[h] = forward(add(up[h], local[step, h]).astype(jnp.bfloat16))
            if step < far or h == 1:
                down[h] = backward(add(down[h], local[chips - step, h]).astype(jnp.bfloat16))

    own = []
    for h in range(2):
        fitted = add(down[h], add(up[h], local[0, h])).astype(jnp.bfloat16)
        own.append(
            jnp.einsum(
                "sjp,pq->sjq", fitted, metric[0], preferred_element_type=jnp.float32
            ).astype(jnp.bfloat16)
        )

    totals = [jnp.zeros((coef.shape[0], tens.shape[2]), jnp.float32)]
    held = {(0, h): own[h] for h in range(2)}
    up, down = list(own), list(own)

    def apply(step, h, **how):
        pieces = []
        for r in sorted({step, (chips - step) % chips}):
            pieces += [held[r, h], across(held[r, h])]
        group = 2 * (far - step) + h
        total, *more = apply_cells(
            (group_starts[group] * half_slots, group, group + 1),
            bounds,
            order,
            cell,
            totals[-1],
            tens,
            pieces,
            capacity * len(pieces) // 2,
            **how,
        )
        totals.append(total)
        return more

    waiting = [(0, 0), (0, 1)]
    for step in range(1, far + 1):
        for h in range(2):
            if step < far or h == 0:
                up[h] = forward(up[h])
            if step < far or h == 1:
                down[h] = backward(down[h])
        if step == far:
            break
        for h in range(2):
            up[h], down[h], totals[-1] = apart((up[h], down[h], totals[-1]))
            apply(*waiting.pop(0))
            up[h], down[h], totals[-1] = apart((up[h], down[h], totals[-1]))
            held[chips - step, h], held[step, h] = up[h], down[h]
            waiting.append((step, h))
    apply(*waiting.pop(0))
    (taken,) = apply(*waiting.pop(0), take=2 * capacity)
    up[0], down[1], totals[-1], taken = apart((up[0], down[1], totals[-1], taken))
    partial_value, = apply_cells(
        (0, 0, 2),
        bounds,
        order,
        cell,
        totals[-1],
        taken,
        [up[0], across(up[0]), down[1], across(down[1])],
        2 * capacity,
        sorted_blocks=True,
    )
    return sum_over_ctr(partial_value)


def slots_body(tens, coef, aux_of, slot_of, metric):
    owners = lax.axis_size("wide")
    block_count = tens.shape[0]
    capacity = max(2, 2 * block_count // owners)
    total_slots = owners * capacity
    half_form = jnp.einsum("jm,bpm->bjp", coef, tens, preferred_element_type=jnp.float32).astype(
        jnp.bfloat16
    )
    target = aux_of[:, 0]
    series = jnp.arange(block_count)
    matches = target[:, None] == target[None, :]
    earlier = series[None, :] < series[:, None]
    ranking = jnp.sum(jnp.where(matches & earlier, 1, 0), axis=1)
    position = target * capacity + ranking
    selector = position[None, :] == jnp.arange(total_slots)[:, None]
    selector_bf = jnp.where(selector, 1.0, 0.0).astype(jnp.bfloat16)
    outgoing = jnp.einsum(
        "kb,bjp->kjp", selector_bf, half_form, preferred_element_type=jnp.float32
    ).astype(jnp.bfloat16)
    slot_tags = jnp.sum(jnp.where(selector, slot_of[None, :] + 1, 0), axis=1)
    received, tags_in = (
        lax.all_to_all(outgoing, "wide", split_axis=0, concat_axis=0, tiled=True),
        lax.all_to_all(slot_tags, "wide", split_axis=0, concat_axis=0, tiled=True),
    )
    slot_onehot = jnp.where(
        tags_in[None, :] == (jnp.arange(OCC_DEV) + 1)[:, None], 1.0, 0.0
    ).astype(jnp.bfloat16)
    fitted = jnp.einsum(
        "sk,kjp->sjp", slot_onehot, received, preferred_element_type=jnp.float32
    ).astype(jnp.bfloat16)
    weighted = jnp.einsum(
        "sjp,pq->sjq", fitted, metric[0], preferred_element_type=jnp.float32
    ).astype(jnp.bfloat16)
    answers = jnp.einsum(
        "sk,sjq->kjq", slot_onehot, weighted, preferred_element_type=jnp.float32
    ).astype(jnp.bfloat16)
    returned = lax.all_to_all(answers, "wide", split_axis=0, concat_axis=0, tiled=True)
    per_block = jnp.einsum(
        "kb,kjq->bjq", selector_bf, returned, preferred_element_type=jnp.float32
    ).astype(jnp.bfloat16)
    partial_value = jnp.einsum("bjq,bqm->jm", per_block, tens, preferred_element_type=jnp.float32)
    return sum_over_ctr(partial_value)


def body(tens, coef, aux_of, slot_of, metric):
    owners, block_count = lax.axis_size("wide"), tens.shape[0]
    dense = owners * OCC_DEV <= 2 * block_count and owners % 4 == 0
    return (cells_body if dense else slots_body)(tens, coef, aux_of, slot_of, metric)


def solution(mesh):
    placed = (
        P(("wide", "ctr"), None, None),
        P(None, "wide"),
        P(("wide", "ctr"), None),
        P(("wide", "ctr")),
        P("wide", None, None),
    )
    return jax.shard_map(
        body, mesh=mesh, in_specs=placed, out_specs=P(None, ("wide", "ctr")), check_vma=False
    )
```

```python
import functools

import jax
import jax.numpy as jnp
from jax import lax
from jax.experimental import pallas as pl
from jax.experimental.pallas import tpu as pltpu
from jax.sharding import PartitionSpec as P

OCC_DEV = 8
GROUP = 4
CHUNKS = 8
KERNEL_VMEM = 28 << 20
APPLY_VMEM = 12 << 20


def ring_place(chip, chips):
    return jnp.where(chip % 2 == 0, chip // 2, chips - 1 - chip // 2)


def ring_pairs(chips, step):
    order = list(range(0, chips, 2)) + list(range(1, chips, 2))[::-1]
    return [
        (2 * order[k] + core, 2 * order[(k + (step, -step)[core]) % chips] + core)
        for k in range(chips)
        for core in range(2)
    ]


def whole(x):
    return pl.BlockSpec(x.shape, lambda i, *_: (0,) * len(x.shape), pipeline_mode=pl.Buffered(1))


def cost(blocks, tens, rows, more):
    width, depth = tens.shape[1:]
    return pl.CostEstimate(
        flops=2 * blocks * rows * width * depth,
        bytes_accessed=2 * blocks * width * depth + more,
        transcendentals=0,
    )


def sum_cells_kernel(sends, cell, again, tens, coef, *refs):
    out, copied, (blocks, rows_in, totals, arrived) = refs[0], refs[1:-4], refs[-4:]
    block_count = tens.shape[0]
    chunk = block_count // CHUNKS
    copies = [pltpu.make_async_copy(coef, rows_in, arrived.at[CHUNKS])]
    for c in range(CHUNKS):
        part = slice(c * chunk, (c + 1) * chunk)
        copies.append(pltpu.make_async_copy(tens.at[part], blocks.at[part], arrived.at[c]))
    for copy in copies:
        copy.start()
    out[...] = jnp.zeros_like(out)
    copies[0].wait()
    for c in range(CHUNKS):
        copies[1 + c].wait()
        for start in range(c * chunk, (c + 1) * chunk, GROUP):
            halves = [
                lax.dot_general(
                    rows_in[...],
                    blocks[b],
                    (((1,), (1,)), ((), ())),
                    preferred_element_type=jnp.float32,
                )
                for b in range(start, start + GROUP)
            ]
            for b, half in zip(range(start, start + GROUP), halves):
                here = cell[b]
                half = half.astype(jnp.bfloat16).astype(jnp.float32)
                total = jnp.where(again[b] != 0, totals[here] + half, half)
                totals[here] = total
                out[here] = total.astype(jnp.bfloat16)
    for send, copy in zip(sends, copied):
        for k, c in enumerate(send):
            copy[k] = out[c]


def sum_cells(cell, again, tens, coef, cells, sends):
    rows, width = coef.shape[0], tens.shape[1]
    outs = [jax.ShapeDtypeStruct((cells, rows, width), jnp.bfloat16)]
    outs += [jax.ShapeDtypeStruct((len(send), rows, width), jnp.bfloat16) for send in sends]
    hbm = pl.BlockSpec(memory_space=pltpu.HBM)
    return pl.pallas_call(
        functools.partial(sum_cells_kernel, sends),
        out_shape=tuple(outs),
        grid_spec=pltpu.PrefetchScalarGridSpec(
            num_scalar_prefetch=2,
            grid=(1,),
            in_specs=[hbm, hbm],
            out_specs=tuple(whole(out) for out in outs),
            scratch_shapes=[
                pltpu.VMEM(tens.shape, tens.dtype),
                pltpu.VMEM(coef.shape, coef.dtype),
                pltpu.VMEM((cells, rows, width), jnp.float32),
                pltpu.SemaphoreType.DMA((CHUNKS + 1,)),
            ],
        ),
        compiler_params=pltpu.CompilerParams(vmem_limit_bytes=KERNEL_VMEM),
        cost_estimate=cost(tens.shape[0], tens, rows, 2 * cells * rows * width),
        name="sum_cells",
    )(
        cell,
        again,
        pltpu.with_memory_space_constraint(tens, pltpu.HBM),
        pltpu.with_memory_space_constraint(coef, pltpu.HBM),
    )


def apply_cells_kernel(group, takes, bounds, order, cell, before, mine, other, first, second, *refs):
    outs, held = refs[:-1], refs[-1]
    half = first.shape[0]
    held[:half], held[half : 2 * half] = first[...], second[...]
    empty = 2 * half
    held[empty] = jnp.zeros(held.shape[1:], held.dtype)
    last = order.shape[1] - 1
    for d, tens in enumerate((mine, other)):
        start, stop = bounds[d, group], bounds[d, group + 1]

        def some(g, total):
            for u in range(GROUP):
                k = start + g * GROUP + u
                b = order[d, jnp.minimum(k, last)]
                here = jnp.where(k < stop, cell[d, b] - 2 * half * group, empty)
                if tens.shape[0] <= last:
                    b = jnp.minimum(k, tens.shape[0] - 1)
                total = total + jnp.dot(held[here], tens[b], preferred_element_type=jnp.float32)
            return total

        outs[0][d] = lax.fori_loop(0, (stop - start + GROUP - 1) // GROUP, some, before[d])
        for k in range(takes):
            outs[1 + d][k] = tens[order[d, k]] if tens.shape[0] > last else tens[k]


def apply_cells(group, tables, before, tens, pieces, takes=0):
    rows, width = pieces[0].shape[1:]
    outs = [jax.ShapeDtypeStruct(before.shape, jnp.float32)]
    if takes:
        outs += [jax.ShapeDtypeStruct((takes, *tens[0].shape[1:]), tens[0].dtype)] * 2
    arrays = [before, *tens, *pieces]
    return pl.pallas_call(
        functools.partial(apply_cells_kernel, group, takes),
        out_shape=tuple(outs),
        grid_spec=pltpu.PrefetchScalarGridSpec(
            num_scalar_prefetch=3,
            grid=(1,),
            in_specs=[whole(array) for array in arrays],
            out_specs=tuple(whole(out) for out in outs),
            scratch_shapes=[pltpu.VMEM((2 * pieces[0].shape[0] + 1, rows, width), jnp.bfloat16)],
        ),
        compiler_params=pltpu.CompilerParams(vmem_limit_bytes=APPLY_VMEM),
        cost_estimate=cost(16, tens[0], rows, 4 * pieces[0].size),
        name="apply_cells",
    )(*tables, *arrays)


def sum_over_ctr(partial_value):
    return lax.psum_scatter(partial_value, "ctr", scatter_dimension=1, tiled=True)


def sum_over_cores_and_ctr(total, owners):
    cores = [(k, k ^ 1) for k in range(owners)]
    if lax.axis_size("ctr") != 2:
        return sum_over_ctr(total[0] + lax.ppermute(total[1], "wide", cores))
    width = total.shape[2] // 2
    low, high = total[:, :, :width], total[:, :, width:]
    lower = lax.axis_index("ctr") == 0
    mine, other = jnp.where(lower, low, high), jnp.where(lower, high, low)
    diagonal = [(2 * a + y, 2 * b + 1 - y) for a, b in cores for y in range(2)]
    parts = (
        lax.ppermute(other[0], "ctr", [(0, 1), (1, 0)]),
        lax.ppermute(other[1], ("wide", "ctr"), diagonal),
        lax.ppermute(mine[1], "wide", cores),
    )
    return (mine[0] + parts[2]) + (parts[0] + parts[1])


def cells_body(tens, coef, aux_of, slot_of, metric):
    owners = lax.axis_size("wide")
    chips = owners // 2
    far = chips // 2
    slots = OCC_DEV
    block_count = tens.shape[0]
    me = lax.axis_index("wide")
    core, place = me % 2, ring_place(me // 2, chips)
    forward = functools.partial(lax.ppermute, axis_name="wide", perm=ring_pairs(chips, 1))
    backward = functools.partial(lax.ppermute, axis_name="wide", perm=ring_pairs(chips, -1))
    across = functools.partial(
        lax.ppermute, axis_name="wide", perm=[(k, k ^ 1) for k in range(owners)]
    )

    half_slots = slots // 2
    long, short = (0, 1), (1, 0)
    turns = [(long, far)] + [(pair, step) for step in range(far - 1, 0, -1) for pair in (short, long)]
    groups = [[(far, 0), (far, 1)]]
    for step in range(far - 1, 0, -1):
        groups += [[(chips - step, pair[0]), (step, pair[1])] for pair in (long, short)]
    groups.append([(0, 0), (0, 1)])
    numbers = {way: k for k, way in enumerate(way for group in groups for way in group)}
    held_cells = len(numbers) * half_slots

    def cell_of(target, slot):
        ahead = ring_place(target // 2, chips) - place
        ahead = jnp.where(target % 2 == 0, ahead, -ahead) % chips
        step = jnp.minimum(ahead, chips - ahead)
        half, back = slot // half_slots, jnp.where(ahead < far, 1, 0)
        between = 2 + (far - 1 - step) * 4 + jnp.where(half == back, 0, 2) + back
        number = jnp.where(step == far, half, jnp.where(step == 0, 4 * far - 2 + half, between))
        return number * half_slots + slot % half_slots

    target = aux_of[:, 0]
    mine_first = jnp.where(target % 2 == core, 0, held_cells)
    cell = cell_of(target, slot_of) + mine_first
    series = jnp.arange(block_count)
    same = (cell[None, :] == cell[:, None]) & (series[None, :] < series[:, None])
    again = jnp.sum(jnp.where(same, 1, 0), axis=1)

    apart = lax.optimization_barrier
    capacity = 2 * block_count // owners
    early = [(r, h) for pair, step in turns[:2] for r, h in ((step, pair[0]), (chips - step, pair[1]))]
    parts = [early, [way for way in numbers if way not in early]]
    sends = []
    for part in parts:
        starts = [held_cells + numbers[way] * half_slots for way in part]
        sends.append([c for start in starts for c in range(start, start + half_slots)])
    sums, *others = sum_cells(cell, again, tens, coef, 2 * held_cells, sends)
    local = {}
    for p, part in enumerate(parts):
        got = across(others[p])
        if p == 0:
            other_names = across(target * slots + slot_of)
            got, other_names, *others[1:] = apart((got, other_names, *others[1:]))
        for k, way in enumerate(part):
            start = numbers[way] * half_slots
            mine = apart(sums[start : start + half_slots])
            other = apart(got[k * half_slots : (k + 1) * half_slots])
            local[way] = mine.astype(jnp.float32) + other.astype(jnp.float32)

    def add(value, held):
        return held if value is None else value.astype(jnp.float32) + held

    up, down, sent = [None, None], [None, None], ()
    for pair, step in turns:
        ahead, back = up[pair[0]], down[pair[1]]
        if ahead is not None:
            ahead, back, *sent = apart((ahead, back, *sent))
        ahead = add(ahead, local[step, pair[0]]).astype(jnp.bfloat16)
        back = add(back, local[chips - step, pair[1]]).astype(jnp.bfloat16)
        sent = (ahead, back)
        up[pair[0]], down[pair[1]] = forward(ahead), backward(back)
        if (pair, step) == turns[6]:
            *sent, tens_out = apart((*sent, tens))
            other_tens = across(tens_out)

    own = []
    for h in range(2):
        fitted = add(down[h], add(up[h], local[0, h])).astype(jnp.bfloat16)
        own.append(
            jnp.einsum(
                "sjp,pq->sjq", fitted, metric[0], preferred_element_type=jnp.float32
            ).astype(jnp.bfloat16)
        )

    tables = []
    for aux, slot in ((target, slot_of), (other_names // slots, other_names % slots)):
        held = jnp.where(aux % 2 == core, cell_of(aux, slot), held_cells)
        key = held * block_count + series
        rank = jnp.sum(jnp.where(key[None, :] < key[:, None], 1, 0), axis=1)
        order = jnp.sum(jnp.where(rank[None, :] == series[:, None], series[None, :], 0), axis=1)
        limits = jnp.arange(len(groups) + 1) * 2 * half_slots
        tables.append((jnp.sum(jnp.where(held[None, :] < limits[:, None], 1, 0), axis=1), order, held))
    tables = [jnp.stack(table) for table in zip(*tables)]

    both = (tens, other_tens)
    total = jnp.zeros((2, coef.shape[0], tens.shape[2]), jnp.float32)
    up, down = [forward(own[h]) for h in range(2)], [backward(own[h]) for h in range(2)]
    uses = [(pair, step) for step in range(1, far) for pair in (long, short)]
    total, *taken = apply_cells(len(groups) - 1, tables, total, both, own, 0 if uses else capacity)
    for pair, step in uses:
        ahead, back = up[pair[0]], down[pair[1]]
        ahead, back, total = apart((ahead, back, total))
        if step + 1 < far or pair == long:
            up[pair[0]], down[pair[1]] = forward(ahead), backward(back)
        group = groups.index([(chips - step, pair[0]), (step, pair[1])])
        takes = capacity if (pair, step) == uses[-1] else 0
        total, *more = apply_cells(group, tables, total, both, [ahead, back], takes)
        taken = more or taken
    (total,) = apply_cells(0, tables, total, taken, [up[0], down[1]])
    return sum_over_cores_and_ctr(total, owners)


def slots_body(tens, coef, aux_of, slot_of, metric):
    owners = lax.axis_size("wide")
    block_count = tens.shape[0]
    capacity = max(2, 2 * block_count // owners)
    total_slots = owners * capacity
    half_form = jnp.einsum("jm,bpm->bjp", coef, tens, preferred_element_type=jnp.float32).astype(
        jnp.bfloat16
    )
    target = aux_of[:, 0]
    series = jnp.arange(block_count)
    matches = target[:, None] == target[None, :]
    earlier = series[None, :] < series[:, None]
    ranking = jnp.sum(jnp.where(matches & earlier, 1, 0), axis=1)
    position = target * capacity + ranking
    selector = position[None, :] == jnp.arange(total_slots)[:, None]
    selector_bf = jnp.where(selector, 1.0, 0.0).astype(jnp.bfloat16)
    outgoing = jnp.einsum(
        "kb,bjp->kjp", selector_bf, half_form, preferred_element_type=jnp.float32
    ).astype(jnp.bfloat16)
    slot_tags = jnp.sum(jnp.where(selector, slot_of[None, :] + 1, 0), axis=1)
    received, tags_in = (
        lax.all_to_all(outgoing, "wide", split_axis=0, concat_axis=0, tiled=True),
        lax.all_to_all(slot_tags, "wide", split_axis=0, concat_axis=0, tiled=True),
    )
    slot_onehot = jnp.where(
        tags_in[None, :] == (jnp.arange(OCC_DEV) + 1)[:, None], 1.0, 0.0
    ).astype(jnp.bfloat16)
    fitted = jnp.einsum(
        "sk,kjp->sjp", slot_onehot, received, preferred_element_type=jnp.float32
    ).astype(jnp.bfloat16)
    weighted = jnp.einsum(
        "sjp,pq->sjq", fitted, metric[0], preferred_element_type=jnp.float32
    ).astype(jnp.bfloat16)
    answers = jnp.einsum(
        "sk,sjq->kjq", slot_onehot, weighted, preferred_element_type=jnp.float32
    ).astype(jnp.bfloat16)
    returned = lax.all_to_all(answers, "wide", split_axis=0, concat_axis=0, tiled=True)
    per_block = jnp.einsum(
        "kb,kjq->bjq", selector_bf, returned, preferred_element_type=jnp.float32
    ).astype(jnp.bfloat16)
    partial_value = jnp.einsum("bjq,bqm->jm", per_block, tens, preferred_element_type=jnp.float32)
    return sum_over_ctr(partial_value)


def body(tens, coef, aux_of, slot_of, metric):
    owners, block_count = lax.axis_size("wide"), tens.shape[0]
    dense = owners * OCC_DEV <= 2 * block_count and owners % 4 == 0
    return (cells_body if dense else slots_body)(tens, coef, aux_of, slot_of, metric)


def solution(mesh):
    placed = (
        P(("wide", "ctr"), None, None),
        P(None, "wide"),
        P(("wide", "ctr"), None),
        P(("wide", "ctr")),
        P("wide", None, None),
    )
    return jax.shard_map(
        body, mesh=mesh, in_specs=placed, out_specs=P(None, ("wide", "ctr")), check_vma=False
    )
```

```python
import functools

import jax
import jax.numpy as jnp
from jax import lax
from jax.experimental import pallas as pl
from jax.experimental.pallas import tpu as pltpu
from jax.sharding import PartitionSpec as P

OCC_DEV = 8
GROUP = 4
CHUNKS = (0, 4, 8, 12, 16)
KERNEL_VMEM = 28 << 20
APPLY_VMEM = 12 << 20


def ring_place(chip, chips):
    return jnp.where(chip % 2 == 0, chip // 2, chips - 1 - chip // 2)


def ring_pairs(chips, step):
    order = list(range(0, chips, 2)) + list(range(1, chips, 2))[::-1]
    return [
        (2 * order[k] + core, 2 * order[(k + (step, -step)[core]) % chips] + core)
        for k in range(chips)
        for core in range(2)
    ]


def whole(x):
    return pl.BlockSpec(x.shape, lambda i, *_: (0,) * len(x.shape), pipeline_mode=pl.Buffered(1))


def cost(blocks, tens, rows, more):
    width, depth = tens.shape[1:]
    return pl.CostEstimate(
        flops=2 * blocks * rows * width * depth,
        bytes_accessed=2 * blocks * width * depth + more,
        transcendentals=0,
    )


def sum_cells_kernel(sends, cell, again, tens, coef, *refs):
    out, copied, (blocks, rows_in, totals, arrived) = refs[0], refs[1:-4], refs[-4:]
    block_count = tens.shape[0]
    edges = [block_count * e // 16 for e in CHUNKS]
    copies = [pltpu.make_async_copy(coef, rows_in, arrived.at[len(edges) - 1])]
    for c, (start, stop) in enumerate(zip(edges, edges[1:])):
        part = slice(start, stop)
        copies.append(pltpu.make_async_copy(tens.at[part], blocks.at[part], arrived.at[c]))
    for copy in copies:
        copy.start()
    out[...] = jnp.zeros_like(out)
    copies[0].wait()
    for c, (first, stop) in enumerate(zip(edges, edges[1:])):
        copies[1 + c].wait()
        for start in range(first, stop, GROUP):
            halves = [
                lax.dot_general(
                    rows_in[...],
                    blocks[b],
                    (((1,), (1,)), ((), ())),
                    preferred_element_type=jnp.float32,
                )
                for b in range(start, start + GROUP)
            ]
            for b, half in zip(range(start, start + GROUP), halves):
                here = cell[b]
                half = half.astype(jnp.bfloat16).astype(jnp.float32)
                total = jnp.where(again[b] != 0, totals[here] + half, half)
                totals[here] = total
                out[here] = total.astype(jnp.bfloat16)
    for send, copy in zip(sends, copied):
        for k, c in enumerate(send):
            copy[k] = out[c]


def sum_cells(cell, again, tens, coef, cells, sends):
    rows, width = coef.shape[0], tens.shape[1]
    outs = [jax.ShapeDtypeStruct((cells, rows, width), jnp.bfloat16)]
    outs += [jax.ShapeDtypeStruct((len(send), rows, width), jnp.bfloat16) for send in sends]
    hbm = pl.BlockSpec(memory_space=pltpu.HBM)
    return pl.pallas_call(
        functools.partial(sum_cells_kernel, sends),
        out_shape=tuple(outs),
        grid_spec=pltpu.PrefetchScalarGridSpec(
            num_scalar_prefetch=2,
            grid=(1,),
            in_specs=[hbm, hbm],
            out_specs=tuple(whole(out) for out in outs),
            scratch_shapes=[
                pltpu.VMEM(tens.shape, tens.dtype),
                pltpu.VMEM(coef.shape, coef.dtype),
                pltpu.VMEM((cells, rows, width), jnp.float32),
                pltpu.SemaphoreType.DMA((len(CHUNKS),)),
            ],
        ),
        compiler_params=pltpu.CompilerParams(vmem_limit_bytes=KERNEL_VMEM),
        cost_estimate=cost(tens.shape[0], tens, rows, 2 * cells * rows * width),
        name="sum_cells",
    )(
        cell,
        again,
        pltpu.with_memory_space_constraint(tens, pltpu.HBM),
        pltpu.with_memory_space_constraint(coef, pltpu.HBM),
    )


def apply_cells_kernel(group, takes, turned, batch, bounds, order, cell, before, mine, other, first, second, *refs):
    outs, held = refs[:-1], refs[-1]
    half = first.shape[0]
    held[:half], held[half : 2 * half] = first[...], second[...]
    empty = 2 * half
    held[empty] = jnp.zeros(held.shape[1:], held.dtype)
    last = order.shape[1] - 1
    for d, tens in enumerate((mine, other)):
        start, stop = bounds[d, group], bounds[d, group + 1]

        def some(g, total):
            for u in range(batch):
                k = start + g * batch + u
                b = order[d, jnp.minimum(k, last)]
                here = jnp.where(k < stop, cell[d, b] - 2 * half * group, empty)
                if tens.shape[0] <= last:
                    b = jnp.minimum(k, tens.shape[0] - 1)
                total = total + jnp.dot(held[here], tens[b], preferred_element_type=jnp.float32)
            return total

        total = lax.fori_loop(0, (stop - start + batch - 1) // batch, some, before[d])
        outs[0][d] = total.T if turned else total
        for k in range(takes):
            outs[1 + d][k] = tens[order[d, k]] if tens.shape[0] > last else tens[k]


def apply_cells(group, tables, before, tens, pieces, takes=0, turned=False):
    rows, width = pieces[0].shape[1:]
    shape = (before.shape[0], before.shape[2], before.shape[1]) if turned else before.shape
    outs = [jax.ShapeDtypeStruct(shape, jnp.float32)]
    if takes:
        outs += [jax.ShapeDtypeStruct((takes, *tens[0].shape[1:]), tens[0].dtype)] * 2
    arrays = [before, *tens, *pieces]
    return pl.pallas_call(
        functools.partial(apply_cells_kernel, group, takes, turned, 2 * GROUP if turned else GROUP),
        out_shape=tuple(outs),
        grid_spec=pltpu.PrefetchScalarGridSpec(
            num_scalar_prefetch=3,
            grid=(1,),
            in_specs=[whole(array) for array in arrays],
            out_specs=tuple(whole(out) for out in outs),
            scratch_shapes=[pltpu.VMEM((2 * pieces[0].shape[0] + 1, rows, width), jnp.bfloat16)],
        ),
        compiler_params=pltpu.CompilerParams(vmem_limit_bytes=APPLY_VMEM),
        cost_estimate=cost(16, tens[0], rows, 4 * pieces[0].size),
        name="apply_cells",
    )(*tables, *arrays)


def sum_over_ctr(partial_value):
    return lax.psum_scatter(partial_value, "ctr", scatter_dimension=1, tiled=True)


def sum_over_cores_and_ctr(total, owners):
    cores = [(k, k ^ 1) for k in range(owners)]
    if lax.axis_size("ctr") != 2:
        return sum_over_ctr((total[0] + lax.ppermute(total[1], "wide", cores)).T)
    width = total.shape[1] // 2
    low, high = total[:, :width], total[:, width:]
    lower = lax.axis_index("ctr") == 0
    mine, other = jnp.where(lower, low, high), jnp.where(lower, high, low)
    diagonal = [(2 * a + y, 2 * b + 1 - y) for a, b in cores for y in range(2)]
    parts = (
        lax.ppermute(other[0], "ctr", [(0, 1), (1, 0)]),
        lax.ppermute(other[1], ("wide", "ctr"), diagonal),
        lax.ppermute(mine[1], "wide", cores),
    )
    return ((mine[0] + parts[2]) + (parts[0] + parts[1])).T


def cells_body(tens, coef, aux_of, slot_of, metric):
    owners = lax.axis_size("wide")
    chips = owners // 2
    far = chips // 2
    slots = OCC_DEV
    block_count = tens.shape[0]
    me = lax.axis_index("wide")
    core, place = me % 2, ring_place(me // 2, chips)
    forward = functools.partial(lax.ppermute, axis_name="wide", perm=ring_pairs(chips, 1))
    backward = functools.partial(lax.ppermute, axis_name="wide", perm=ring_pairs(chips, -1))
    across = functools.partial(
        lax.ppermute, axis_name="wide", perm=[(k, k ^ 1) for k in range(owners)]
    )

    half_slots = slots // 2
    long, short = (0, 1), (1, 0)
    turns = [(long, far)] + [(pair, step) for step in range(far - 1, 0, -1) for pair in (short, long)]
    groups = [[(far, 0), (far, 1)]]
    for step in range(far - 1, 0, -1):
        groups += [[(chips - step, pair[0]), (step, pair[1])] for pair in (long, short)]
    groups.append([(0, 0), (0, 1)])
    numbers = {way: k for k, way in enumerate(way for group in groups for way in group)}
    held_cells = len(numbers) * half_slots

    def cell_of(target, slot):
        ahead = ring_place(target // 2, chips) - place
        ahead = jnp.where(target % 2 == 0, ahead, -ahead) % chips
        step = jnp.minimum(ahead, chips - ahead)
        half, back = slot // half_slots, jnp.where(ahead < far, 1, 0)
        between = 2 + (far - 1 - step) * 4 + jnp.where(half == back, 0, 2) + back
        number = jnp.where(step == far, half, jnp.where(step == 0, 4 * far - 2 + half, between))
        return number * half_slots + slot % half_slots

    target = aux_of[:, 0]
    mine_first = jnp.where(target % 2 == core, 0, held_cells)
    cell = cell_of(target, slot_of) + mine_first
    series = jnp.arange(block_count)
    same = (cell[None, :] == cell[:, None]) & (series[None, :] < series[:, None])
    again = jnp.sum(jnp.where(same, 1, 0), axis=1)

    apart = lax.optimization_barrier
    capacity = 2 * block_count // owners
    early = [(r, h) for pair, step in turns[:2] for r, h in ((step, pair[0]), (chips - step, pair[1]))]
    parts = [early, [way for way in numbers if way not in early]]
    sends = []
    for part in parts:
        starts = [held_cells + numbers[way] * half_slots for way in part]
        sends.append([c for start in starts for c in range(start, start + half_slots)])
    sums, *others = sum_cells(cell, again, tens, coef, 2 * held_cells, sends)
    local = {}
    for p, part in enumerate(parts):
        got = across(others[p])
        if p == 0:
            other_names = across(target * slots + slot_of)
            got, other_names, *others[1:] = apart((got, other_names, *others[1:]))
        if p == 1:
            got, tens_out = apart((got, tens))
            other_tens = across(tens_out)
        for k, way in enumerate(part):
            start = numbers[way] * half_slots
            mine = apart(sums[start : start + half_slots])
            other = apart(got[k * half_slots : (k + 1) * half_slots])
            local[way] = mine.astype(jnp.float32) + other.astype(jnp.float32)

    def add(value, held):
        return held if value is None else value.astype(jnp.float32) + held

    up, down, sent = [None, None], [None, None], ()
    for pair, step in turns:
        ahead, back = up[pair[0]], down[pair[1]]
        if ahead is not None:
            ahead, back, *sent = apart((ahead, back, *sent))
        ahead = add(ahead, local[step, pair[0]]).astype(jnp.bfloat16)
        back = add(back, local[chips - step, pair[1]]).astype(jnp.bfloat16)
        sent = (ahead, back)
        up[pair[0]], down[pair[1]] = forward(ahead), backward(back)

    own = []
    for h in range(2):
        fitted = add(down[h], add(up[h], local[0, h])).astype(jnp.bfloat16)
        own.append(
            jnp.einsum(
                "sjp,pq->sjq", fitted, metric[0], preferred_element_type=jnp.float32
            ).astype(jnp.bfloat16)
        )

    tables = []
    for aux, slot in ((target, slot_of), (other_names // slots, other_names % slots)):
        held = jnp.where(aux % 2 == core, cell_of(aux, slot), held_cells)
        key = held * block_count + series
        rank = jnp.sum(jnp.where(key[None, :] < key[:, None], 1, 0), axis=1)
        order = jnp.sum(jnp.where(rank[None, :] == series[:, None], series[None, :], 0), axis=1)
        limits = jnp.arange(len(groups) + 1) * 2 * half_slots
        tables.append((jnp.sum(jnp.where(held[None, :] < limits[:, None], 1, 0), axis=1), order, held))
    tables = [jnp.stack(table) for table in zip(*tables)]

    both = (tens, other_tens)
    total = jnp.zeros((2, coef.shape[0], tens.shape[2]), jnp.float32)
    up, down = [forward(own[h]) for h in range(2)], [backward(own[h]) for h in range(2)]
    uses = [(pair, step) for step in range(1, far) for pair in (long, short)]
    total, *taken = apply_cells(len(groups) - 1, tables, total, both, own, 0 if uses else capacity)
    for pair, step in uses:
        ahead, back = up[pair[0]], down[pair[1]]
        ahead, back, total = apart((ahead, back, total))
        if step + 1 < far or pair == long:
            up[pair[0]], down[pair[1]] = forward(ahead), backward(back)
        group = groups.index([(chips - step, pair[0]), (step, pair[1])])
        takes = capacity if (pair, step) == uses[-1] else 0
        total, *more = apply_cells(group, tables, total, both, [ahead, back], takes)
        taken = more or taken
    (total,) = apply_cells(0, tables, total, taken, [up[0], down[1]], turned=True)
    return sum_over_cores_and_ctr(total, owners)


def slots_body(tens, coef, aux_of, slot_of, metric):
    owners = lax.axis_size("wide")
    block_count = tens.shape[0]
    capacity = max(2, 2 * block_count // owners)
    total_slots = owners * capacity
    half_form = jnp.einsum("jm,bpm->bjp", coef, tens, preferred_element_type=jnp.float32).astype(
        jnp.bfloat16
    )
    target = aux_of[:, 0]
    series = jnp.arange(block_count)
    matches = target[:, None] == target[None, :]
    earlier = series[None, :] < series[:, None]
    ranking = jnp.sum(jnp.where(matches & earlier, 1, 0), axis=1)
    position = target * capacity + ranking
    selector = position[None, :] == jnp.arange(total_slots)[:, None]
    selector_bf = jnp.where(selector, 1.0, 0.0).astype(jnp.bfloat16)
    outgoing = jnp.einsum(
        "kb,bjp->kjp", selector_bf, half_form, preferred_element_type=jnp.float32
    ).astype(jnp.bfloat16)
    slot_tags = jnp.sum(jnp.where(selector, slot_of[None, :] + 1, 0), axis=1)
    received, tags_in = (
        lax.all_to_all(outgoing, "wide", split_axis=0, concat_axis=0, tiled=True),
        lax.all_to_all(slot_tags, "wide", split_axis=0, concat_axis=0, tiled=True),
    )
    slot_onehot = jnp.where(
        tags_in[None, :] == (jnp.arange(OCC_DEV) + 1)[:, None], 1.0, 0.0
    ).astype(jnp.bfloat16)
    fitted = jnp.einsum(
        "sk,kjp->sjp", slot_onehot, received, preferred_element_type=jnp.float32
    ).astype(jnp.bfloat16)
    weighted = jnp.einsum(
        "sjp,pq->sjq", fitted, metric[0], preferred_element_type=jnp.float32
    ).astype(jnp.bfloat16)
    answers = jnp.einsum(
        "sk,sjq->kjq", slot_onehot, weighted, preferred_element_type=jnp.float32
    ).astype(jnp.bfloat16)
    returned = lax.all_to_all(answers, "wide", split_axis=0, concat_axis=0, tiled=True)
    per_block = jnp.einsum(
        "kb,kjq->bjq", selector_bf, returned, preferred_element_type=jnp.float32
    ).astype(jnp.bfloat16)
    partial_value = jnp.einsum("bjq,bqm->jm", per_block, tens, preferred_element_type=jnp.float32)
    return sum_over_ctr(partial_value)


def body(tens, coef, aux_of, slot_of, metric):
    owners, block_count = lax.axis_size("wide"), tens.shape[0]
    dense = owners * OCC_DEV <= 2 * block_count and owners % 4 == 0 and block_count % 64 == 0
    return (cells_body if dense else slots_body)(tens, coef, aux_of, slot_of, metric)


def solution(mesh):
    placed = (
        P(("wide", "ctr"), None, None),
        P(None, "wide"),
        P(("wide", "ctr"), None),
        P(("wide", "ctr")),
        P("wide", None, None),
    )
    return jax.shard_map(
        body, mesh=mesh, in_specs=placed, out_specs=P(None, ("wide", "ctr")), check_vma=False
    )
```

```python
import functools

import jax
import jax.numpy as jnp
from jax import lax
from jax.experimental import pallas as pl
from jax.experimental.pallas import tpu as pltpu
from jax.sharding import PartitionSpec as P

OCC_DEV = 8
GROUP = 4
CHUNKS = (0, 4, 8, 12, 16)
KERNEL_VMEM = 28 << 20
APPLY_VMEM = 12 << 20


def ring_place(chip, chips):
    return jnp.where(chip % 2 == 0, chip // 2, chips - 1 - chip // 2)


def ring_pairs(chips, step):
    order = list(range(0, chips, 2)) + list(range(1, chips, 2))[::-1]
    return [
        (2 * order[k] + core, 2 * order[(k + (step, -step)[core]) % chips] + core)
        for k in range(chips)
        for core in range(2)
    ]


def whole(x):
    return pl.BlockSpec(x.shape, lambda i, *_: (0,) * len(x.shape), pipeline_mode=pl.Buffered(1))


def cost(blocks, tens, rows, more):
    width, depth = tens.shape[1:]
    return pl.CostEstimate(
        flops=2 * blocks * rows * width * depth,
        bytes_accessed=2 * blocks * width * depth + more,
        transcendentals=0,
    )


def sum_cells_kernel(sends, cell, again, tens, coef, *refs):
    out, copied, (blocks, rows_in, totals, arrived) = refs[0], refs[1:-4], refs[-4:]
    block_count = tens.shape[0]
    edges = [block_count * e // 16 for e in CHUNKS]
    copies = [pltpu.make_async_copy(coef, rows_in, arrived.at[len(edges) - 1])]
    for c, (start, stop) in enumerate(zip(edges, edges[1:])):
        part = slice(start, stop)
        copies.append(pltpu.make_async_copy(tens.at[part], blocks.at[part], arrived.at[c]))
    for copy in copies:
        copy.start()
    out[...] = jnp.zeros_like(out)
    copies[0].wait()
    for c, (first, stop) in enumerate(zip(edges, edges[1:])):
        copies[1 + c].wait()
        for start in range(first, stop, GROUP):
            width = blocks.shape[1]
            group = blocks[start : start + GROUP].reshape(GROUP * width, blocks.shape[2])
            product = lax.dot_general(
                rows_in[...], group, (((1,), (1,)), ((), ())), preferred_element_type=jnp.float32
            )
            halves = [product[:, u * width : (u + 1) * width] for u in range(GROUP)]
            for b, half in zip(range(start, start + GROUP), halves):
                here = cell[b]
                half = half.astype(jnp.bfloat16).astype(jnp.float32)
                total = jnp.where(again[b] != 0, totals[here] + half, half)
                totals[here] = total
                out[here] = total.astype(jnp.bfloat16)
    for send, copy in zip(sends, copied):
        for k, c in enumerate(send):
            copy[k] = out[c]


def sum_cells(cell, again, tens, coef, cells, sends):
    rows, width = coef.shape[0], tens.shape[1]
    outs = [jax.ShapeDtypeStruct((cells, rows, width), jnp.bfloat16)]
    outs += [jax.ShapeDtypeStruct((len(send), rows, width), jnp.bfloat16) for send in sends]
    hbm = pl.BlockSpec(memory_space=pltpu.HBM)
    return pl.pallas_call(
        functools.partial(sum_cells_kernel, sends),
        out_shape=tuple(outs),
        grid_spec=pltpu.PrefetchScalarGridSpec(
            num_scalar_prefetch=2,
            grid=(1,),
            in_specs=[hbm, hbm],
            out_specs=tuple(whole(out) for out in outs),
            scratch_shapes=[
                pltpu.VMEM(tens.shape, tens.dtype),
                pltpu.VMEM(coef.shape, coef.dtype),
                pltpu.VMEM((cells, rows, width), jnp.float32),
                pltpu.SemaphoreType.DMA((len(CHUNKS),)),
            ],
        ),
        compiler_params=pltpu.CompilerParams(vmem_limit_bytes=KERNEL_VMEM),
        cost_estimate=cost(tens.shape[0], tens, rows, 2 * cells * rows * width),
        name="sum_cells",
    )(
        cell,
        again,
        pltpu.with_memory_space_constraint(tens, pltpu.HBM),
        pltpu.with_memory_space_constraint(coef, pltpu.HBM),
    )


def apply_cells_kernel(group, takes, turned, batch, bounds, order, cell, before, mine, other, first, second, *refs):
    outs, held = refs[:-1], refs[-1]
    half = first.shape[0]
    held[:half], held[half : 2 * half] = first[...], second[...]
    empty = 2 * half
    held[empty] = jnp.zeros(held.shape[1:], held.dtype)
    last = order.shape[1] - 1
    for d, tens in enumerate((mine, other)):
        start, stop = bounds[d, group], bounds[d, group + 1]

        def some(g, total):
            for u in range(batch):
                k = start + g * batch + u
                b = order[d, jnp.minimum(k, last)]
                here = jnp.where(k < stop, cell[d, b] - 2 * half * group, empty)
                if tens.shape[0] <= last:
                    b = jnp.minimum(k, tens.shape[0] - 1)
                total = total + jnp.dot(held[here], tens[b], preferred_element_type=jnp.float32)
            return total

        total = lax.fori_loop(0, (stop - start + batch - 1) // batch, some, before[d])
        outs[0][d] = total.T if turned else total
        for k in range(takes):
            outs[1 + d][k] = tens[order[d, k]] if tens.shape[0] > last else tens[k]


def apply_cells(group, tables, before, tens, pieces, takes=0, turned=False):
    rows, width = pieces[0].shape[1:]
    shape = (before.shape[0], before.shape[2], before.shape[1]) if turned else before.shape
    outs = [jax.ShapeDtypeStruct(shape, jnp.float32)]
    if takes:
        outs += [jax.ShapeDtypeStruct((takes, *tens[0].shape[1:]), tens[0].dtype)] * 2
    arrays = [before, *tens, *pieces]
    return pl.pallas_call(
        functools.partial(apply_cells_kernel, group, takes, turned, 2 * GROUP if turned else GROUP),
        out_shape=tuple(outs),
        grid_spec=pltpu.PrefetchScalarGridSpec(
            num_scalar_prefetch=3,
            grid=(1,),
            in_specs=[whole(array) for array in arrays],
            out_specs=tuple(whole(out) for out in outs),
            scratch_shapes=[pltpu.VMEM((2 * pieces[0].shape[0] + 1, rows, width), jnp.bfloat16)],
        ),
        compiler_params=pltpu.CompilerParams(vmem_limit_bytes=APPLY_VMEM),
        cost_estimate=cost(16, tens[0], rows, 4 * pieces[0].size),
        name="apply_cells",
    )(*tables, *arrays)


def sum_over_ctr(partial_value):
    return lax.psum_scatter(partial_value, "ctr", scatter_dimension=1, tiled=True)


def sum_over_cores_and_ctr(total, owners):
    cores = [(k, k ^ 1) for k in range(owners)]
    if lax.axis_size("ctr") != 2:
        return sum_over_ctr((total[0] + lax.ppermute(total[1], "wide", cores)).T)
    width = total.shape[1] // 2
    low, high = total[:, :width], total[:, width:]
    lower = lax.axis_index("ctr") == 0
    mine, other = jnp.where(lower, low, high), jnp.where(lower, high, low)
    diagonal = [(2 * a + y, 2 * b + 1 - y) for a, b in cores for y in range(2)]
    parts = (
        lax.ppermute(other[0], "ctr", [(0, 1), (1, 0)]),
        lax.ppermute(other[1], ("wide", "ctr"), diagonal),
        lax.ppermute(mine[1], "wide", cores),
    )
    return ((mine[0] + parts[2]) + (parts[0] + parts[1])).T


def cells_body(tens, coef, aux_of, slot_of, metric):
    owners = lax.axis_size("wide")
    chips = owners // 2
    far = chips // 2
    slots = OCC_DEV
    block_count = tens.shape[0]
    me = lax.axis_index("wide")
    core, place = me % 2, ring_place(me // 2, chips)
    forward = functools.partial(lax.ppermute, axis_name="wide", perm=ring_pairs(chips, 1))
    backward = functools.partial(lax.ppermute, axis_name="wide", perm=ring_pairs(chips, -1))
    across = functools.partial(
        lax.ppermute, axis_name="wide", perm=[(k, k ^ 1) for k in range(owners)]
    )

    half_slots = slots // 2
    long, short = (0, 1), (1, 0)
    turns = [(long, far)] + [(pair, step) for step in range(far - 1, 0, -1) for pair in (short, long)]
    groups = [[(far, 0), (far, 1)]]
    for step in range(far - 1, 0, -1):
        groups += [[(chips - step, pair[0]), (step, pair[1])] for pair in (long, short)]
    groups.append([(0, 0), (0, 1)])
    numbers = {way: k for k, way in enumerate(way for group in groups for way in group)}
    held_cells = len(numbers) * half_slots

    def cell_of(target, slot):
        ahead = ring_place(target // 2, chips) - place
        ahead = jnp.where(target % 2 == 0, ahead, -ahead) % chips
        step = jnp.minimum(ahead, chips - ahead)
        half, back = slot // half_slots, jnp.where(ahead < far, 1, 0)
        between = 2 + (far - 1 - step) * 4 + jnp.where(half == back, 0, 2) + back
        number = jnp.where(step == far, half, jnp.where(step == 0, 4 * far - 2 + half, between))
        return number * half_slots + slot % half_slots

    target = aux_of[:, 0]
    mine_first = jnp.where(target % 2 == core, 0, held_cells)
    cell = cell_of(target, slot_of) + mine_first
    series = jnp.arange(block_count)
    same = (cell[None, :] == cell[:, None]) & (series[None, :] < series[:, None])
    again = jnp.sum(jnp.where(same, 1, 0), axis=1)

    apart = lax.optimization_barrier
    capacity = 2 * block_count // owners
    early = [(r, h) for pair, step in turns[:1] for r, h in ((step, pair[0]), (chips - step, pair[1]))]
    parts = [early, [way for way in numbers if way not in early]]
    sends = []
    for part in parts:
        starts = [held_cells + numbers[way] * half_slots for way in part]
        sends.append([c for start in starts for c in range(start, start + half_slots)])
    starts = [numbers[way] * half_slots for way in early]
    kept = [[c for c in range(start, start + half_slots)] for start in starts]
    sums, *others = sum_cells(cell, again, tens, coef, 2 * held_cells, sends + kept)
    local = {}
    for p, part in enumerate(parts):
        got = across(others[p])
        if p == 0:
            other_names = across(target * slots + slot_of)
            got, other_names, others[1] = apart((got, other_names, others[1]))
        if p == 1:
            got, tens_out = apart((got, tens))
            other_tens = across(tens_out)
        for k, way in enumerate(part):
            start = numbers[way] * half_slots
            mine = others[2 + k] if p == 0 else apart(sums[start : start + half_slots])
            other = apart(got[k * half_slots : (k + 1) * half_slots])
            local[way] = mine.astype(jnp.float32) + other.astype(jnp.float32)

    def add(value, held):
        return held if value is None else value.astype(jnp.float32) + held

    up, down, sent = [None, None], [None, None], ()
    for pair, step in turns:
        ahead, back = up[pair[0]], down[pair[1]]
        if ahead is not None:
            ahead, back, *sent = apart((ahead, back, *sent))
            if (pair, step) == turns[3]:
                ahead, names, other_names = apart((ahead, target * slots + slot_of, other_names))
        ahead = add(ahead, local[step, pair[0]]).astype(jnp.bfloat16)
        back = add(back, local[chips - step, pair[1]]).astype(jnp.bfloat16)
        sent = (ahead, back)
        up[pair[0]], down[pair[1]] = forward(ahead), backward(back)

    own = []
    for h in range(2):
        fitted = add(down[h], add(up[h], local[0, h])).astype(jnp.bfloat16)
        own.append(
            jnp.einsum(
                "sjp,pq->sjq", fitted, metric[0], preferred_element_type=jnp.float32
            ).astype(jnp.bfloat16)
        )

    tables = []
    for aux, slot in ((n // slots, n % slots) for n in (names, other_names)):
        held = jnp.where(aux % 2 == core, cell_of(aux, slot), held_cells)
        key = held * block_count + series
        rank = jnp.sum(jnp.where(key[None, :] < key[:, None], 1, 0), axis=1)
        order = jnp.sum(jnp.where(rank[None, :] == series[:, None], series[None, :], 0), axis=1)
        limits = jnp.arange(len(groups) + 1) * 2 * half_slots
        tables.append((jnp.sum(jnp.where(held[None, :] < limits[:, None], 1, 0), axis=1), order, held))
    tables = [jnp.stack(table) for table in zip(*tables)]

    both = (tens, other_tens)
    total = jnp.zeros((2, coef.shape[0], tens.shape[2]), jnp.float32)
    up, down = [forward(own[h]) for h in range(2)], [backward(own[h]) for h in range(2)]
    uses = [(pair, step) for step in range(1, far) for pair in (long, short)]
    total, *taken = apply_cells(len(groups) - 1, tables, total, both, own, 0 if uses else capacity)
    for pair, step in uses:
        ahead, back = up[pair[0]], down[pair[1]]
        ahead, back, total = apart((ahead, back, total))
        if step + 1 < far or pair == long:
            up[pair[0]], down[pair[1]] = forward(ahead), backward(back)
        group = groups.index([(chips - step, pair[0]), (step, pair[1])])
        takes = capacity if (pair, step) == uses[-1] else 0
        total, *more = apply_cells(group, tables, total, both, [ahead, back], takes)
        taken = more or taken
    (total,) = apply_cells(0, tables, total, taken, [up[0], down[1]], turned=True)
    return sum_over_cores_and_ctr(total, owners)


def slots_body(tens, coef, aux_of, slot_of, metric):
    owners = lax.axis_size("wide")
    block_count = tens.shape[0]
    capacity = max(2, 2 * block_count // owners)
    total_slots = owners * capacity
    half_form = jnp.einsum("jm,bpm->bjp", coef, tens, preferred_element_type=jnp.float32).astype(
        jnp.bfloat16
    )
    target = aux_of[:, 0]
    series = jnp.arange(block_count)
    matches = target[:, None] == target[None, :]
    earlier = series[None, :] < series[:, None]
    ranking = jnp.sum(jnp.where(matches & earlier, 1, 0), axis=1)
    position = target * capacity + ranking
    selector = position[None, :] == jnp.arange(total_slots)[:, None]
    selector_bf = jnp.where(selector, 1.0, 0.0).astype(jnp.bfloat16)
    outgoing = jnp.einsum(
        "kb,bjp->kjp", selector_bf, half_form, preferred_element_type=jnp.float32
    ).astype(jnp.bfloat16)
    slot_tags = jnp.sum(jnp.where(selector, slot_of[None, :] + 1, 0), axis=1)
    received, tags_in = (
        lax.all_to_all(outgoing, "wide", split_axis=0, concat_axis=0, tiled=True),
        lax.all_to_all(slot_tags, "wide", split_axis=0, concat_axis=0, tiled=True),
    )
    slot_onehot = jnp.where(
        tags_in[None, :] == (jnp.arange(OCC_DEV) + 1)[:, None], 1.0, 0.0
    ).astype(jnp.bfloat16)
    fitted = jnp.einsum(
        "sk,kjp->sjp", slot_onehot, received, preferred_element_type=jnp.float32
    ).astype(jnp.bfloat16)
    weighted = jnp.einsum(
        "sjp,pq->sjq", fitted, metric[0], preferred_element_type=jnp.float32
    ).astype(jnp.bfloat16)
    answers = jnp.einsum(
        "sk,sjq->kjq", slot_onehot, weighted, preferred_element_type=jnp.float32
    ).astype(jnp.bfloat16)
    returned = lax.all_to_all(answers, "wide", split_axis=0, concat_axis=0, tiled=True)
    per_block = jnp.einsum(
        "kb,kjq->bjq", selector_bf, returned, preferred_element_type=jnp.float32
    ).astype(jnp.bfloat16)
    partial_value = jnp.einsum("bjq,bqm->jm", per_block, tens, preferred_element_type=jnp.float32)
    return sum_over_ctr(partial_value)


def body(tens, coef, aux_of, slot_of, metric):
    owners, block_count = lax.axis_size("wide"), tens.shape[0]
    dense = owners * OCC_DEV <= 2 * block_count and owners % 4 == 0 and block_count % 64 == 0
    return (cells_body if dense else slots_body)(tens, coef, aux_of, slot_of, metric)


def solution(mesh):
    placed = (
        P(("wide", "ctr"), None, None),
        P(None, "wide"),
        P(("wide", "ctr"), None),
        P(("wide", "ctr")),
        P("wide", None, None),
    )
    return jax.shard_map(
        body, mesh=mesh, in_specs=placed, out_specs=P(None, ("wide", "ctr")), check_vma=False
    )
```

```python
import functools

import jax
import jax.numpy as jnp
from jax import lax
from jax.experimental import pallas as pl
from jax.experimental.pallas import tpu as pltpu
from jax.sharding import PartitionSpec as P

OCC_DEV = 8
GROUP = 4
CHUNKS = (0, 4, 8, 12, 16)
KERNEL_VMEM = 28 << 20
APPLY_VMEM = 12 << 20


def ring_place(chip, chips):
    return jnp.where(chip % 2 == 0, chip // 2, chips - 1 - chip // 2)


def ring_pairs(chips, step):
    order = list(range(0, chips, 2)) + list(range(1, chips, 2))[::-1]
    return [
        (2 * order[k] + core, 2 * order[(k + (step, -step)[core]) % chips] + core)
        for k in range(chips)
        for core in range(2)
    ]


def whole(x):
    return pl.BlockSpec(x.shape, lambda i, *_: (0,) * len(x.shape), pipeline_mode=pl.Buffered(1))


def cost(blocks, tens, rows, more):
    width, depth = tens.shape[1:]
    return pl.CostEstimate(
        flops=2 * blocks * rows * width * depth,
        bytes_accessed=2 * blocks * width * depth + more,
        transcendentals=0,
    )


def sum_cells_kernel(sends, cell, again, tens, coef, *refs):
    out, copied, (blocks, rows_in, totals, arrived) = refs[0], refs[1:-4], refs[-4:]
    block_count = tens.shape[0]
    edges = [block_count * e // 16 for e in CHUNKS]
    copies = [pltpu.make_async_copy(coef, rows_in, arrived.at[len(edges) - 1])]
    for c, (start, stop) in enumerate(zip(edges, edges[1:])):
        part = slice(start, stop)
        copies.append(pltpu.make_async_copy(tens.at[part], blocks.at[part], arrived.at[c]))
    for copy in copies:
        copy.start()
    out[...] = jnp.zeros_like(out)
    copies[0].wait()
    for c, (first, stop) in enumerate(zip(edges, edges[1:])):
        copies[1 + c].wait()
        for start in range(first, stop, GROUP):
            width = blocks.shape[1]
            group = blocks[start : start + GROUP].reshape(GROUP * width, blocks.shape[2])
            product = lax.dot_general(
                rows_in[...], group, (((1,), (1,)), ((), ())), preferred_element_type=jnp.float32
            )
            halves = [product[:, u * width : (u + 1) * width] for u in range(GROUP)]
            for b, half in zip(range(start, start + GROUP), halves):
                here = cell[b]
                half = half.astype(jnp.bfloat16).astype(jnp.float32)
                total = jnp.where(again[b] != 0, totals[here] + half, half)
                totals[here] = total
                out[here] = total.astype(jnp.bfloat16)
    for send, copy in zip(sends, copied):
        for k, c in enumerate(send):
            copy[k] = out[c]


def sum_cells(cell, again, tens, coef, cells, sends):
    rows, width = coef.shape[0], tens.shape[1]
    outs = [jax.ShapeDtypeStruct((cells, rows, width), jnp.bfloat16)]
    outs += [jax.ShapeDtypeStruct((len(send), rows, width), jnp.bfloat16) for send in sends]
    hbm = pl.BlockSpec(memory_space=pltpu.HBM)
    return pl.pallas_call(
        functools.partial(sum_cells_kernel, sends),
        out_shape=tuple(outs),
        grid_spec=pltpu.PrefetchScalarGridSpec(
            num_scalar_prefetch=2,
            grid=(1,),
            in_specs=[hbm, hbm],
            out_specs=tuple(whole(out) for out in outs),
            scratch_shapes=[
                pltpu.VMEM(tens.shape, tens.dtype),
                pltpu.VMEM(coef.shape, coef.dtype),
                pltpu.VMEM((cells, rows, width), jnp.float32),
                pltpu.SemaphoreType.DMA((len(CHUNKS),)),
            ],
        ),
        compiler_params=pltpu.CompilerParams(vmem_limit_bytes=KERNEL_VMEM),
        cost_estimate=cost(tens.shape[0], tens, rows, 2 * cells * rows * width),
        name="sum_cells",
    )(
        cell,
        again,
        pltpu.with_memory_space_constraint(tens, pltpu.HBM),
        pltpu.with_memory_space_constraint(coef, pltpu.HBM),
    )


def apply_cells_kernel(group, takes, turned, batch, bounds, order, cell, before, mine, other, first, second, *refs):
    outs, held = refs[:-1], refs[-1]
    half = first.shape[0]
    held[:half], held[half : 2 * half] = first[...], second[...]
    empty = 2 * half
    held[empty] = jnp.zeros(held.shape[1:], held.dtype)
    last = order.shape[1] - 1
    for d, tens in enumerate((mine, other)):
        start, stop = bounds[d, group], bounds[d, group + 1]

        def some(g, total):
            for u in range(batch):
                k = start + g * batch + u
                b = order[d, jnp.minimum(k, last)]
                here = jnp.where(k < stop, cell[d, b] - 2 * half * group, empty)
                if tens.shape[0] <= last:
                    b = jnp.minimum(k, tens.shape[0] - 1)
                total = total + jnp.dot(held[here], tens[b], preferred_element_type=jnp.float32)
            return total

        total = lax.fori_loop(0, (stop - start + batch - 1) // batch, some, before[d])
        outs[0][d] = total.T if turned else total
        for k in range(takes):
            outs[1 + d][k] = tens[order[d, k]] if tens.shape[0] > last else tens[k]


def apply_cells(group, tables, before, tens, pieces, takes=0, turned=False):
    rows, width = pieces[0].shape[1:]
    shape = (before.shape[0], before.shape[2], before.shape[1]) if turned else before.shape
    outs = [jax.ShapeDtypeStruct(shape, jnp.float32)]
    if takes:
        outs += [jax.ShapeDtypeStruct((takes, *tens[0].shape[1:]), tens[0].dtype)] * 2
    arrays = [before, *tens, *pieces]
    return pl.pallas_call(
        functools.partial(apply_cells_kernel, group, takes, turned, 2 * GROUP if turned else GROUP),
        out_shape=tuple(outs),
        grid_spec=pltpu.PrefetchScalarGridSpec(
            num_scalar_prefetch=3,
            grid=(1,),
            in_specs=[whole(array) for array in arrays],
            out_specs=tuple(whole(out) for out in outs),
            scratch_shapes=[pltpu.VMEM((2 * pieces[0].shape[0] + 1, rows, width), jnp.bfloat16)],
        ),
        compiler_params=pltpu.CompilerParams(vmem_limit_bytes=APPLY_VMEM),
        cost_estimate=cost(16, tens[0], rows, 4 * pieces[0].size),
        name="apply_cells",
    )(*tables, *arrays)


def sum_over_ctr(partial_value):
    return lax.psum_scatter(partial_value, "ctr", scatter_dimension=1, tiled=True)


def sum_over_cores_and_ctr(total, owners):
    cores = [(k, k ^ 1) for k in range(owners)]
    if lax.axis_size("ctr") != 2:
        return sum_over_ctr((total[0] + lax.ppermute(total[1], "wide", cores)).T)
    width = total.shape[1] // 2
    whole_sum = total[0] + lax.ppermute(total[1], "wide", cores)
    low, high = whole_sum[:width], whole_sum[width:]
    lower = lax.axis_index("ctr") == 0
    mine, other = jnp.where(lower, low, high), jnp.where(lower, high, low)
    return (mine + lax.ppermute(other, "ctr", [(0, 1), (1, 0)])).T


def cells_body(tens, coef, aux_of, slot_of, metric):
    owners = lax.axis_size("wide")
    chips = owners // 2
    far = chips // 2
    slots = OCC_DEV
    block_count = tens.shape[0]
    me = lax.axis_index("wide")
    core, place = me % 2, ring_place(me // 2, chips)
    forward = functools.partial(lax.ppermute, axis_name="wide", perm=ring_pairs(chips, 1))
    backward = functools.partial(lax.ppermute, axis_name="wide", perm=ring_pairs(chips, -1))
    across = functools.partial(
        lax.ppermute, axis_name="wide", perm=[(k, k ^ 1) for k in range(owners)]
    )

    half_slots = slots // 2
    long, short = (0, 1), (1, 0)
    turns = [(long, far)] + [(pair, step) for step in range(far - 1, 0, -1) for pair in (short, long)]
    groups = [[(far, 0), (far, 1)]]
    for step in range(far - 1, 0, -1):
        groups += [[(chips - step, pair[0]), (step, pair[1])] for pair in (long, short)]
    groups.append([(0, 0), (0, 1)])
    numbers = {way: k for k, way in enumerate(way for group in groups for way in group)}
    held_cells = len(numbers) * half_slots

    def cell_of(target, slot):
        ahead = ring_place(target // 2, chips) - place
        ahead = jnp.where(target % 2 == 0, ahead, -ahead) % chips
        step = jnp.minimum(ahead, chips - ahead)
        half, back = slot // half_slots, jnp.where(ahead < far, 1, 0)
        between = 2 + (far - 1 - step) * 4 + jnp.where(half == back, 0, 2) + back
        number = jnp.where(step == far, half, jnp.where(step == 0, 4 * far - 2 + half, between))
        return number * half_slots + slot % half_slots

    target = aux_of[:, 0]
    mine_first = jnp.where(target % 2 == core, 0, held_cells)
    cell = cell_of(target, slot_of) + mine_first
    series = jnp.arange(block_count)
    same = (cell[None, :] == cell[:, None]) & (series[None, :] < series[:, None])
    again = jnp.sum(jnp.where(same, 1, 0), axis=1)

    apart = lax.optimization_barrier
    capacity = 2 * block_count // owners
    early = [(r, h) for pair, step in turns[:1] for r, h in ((step, pair[0]), (chips - step, pair[1]))]
    parts = [early, [way for way in numbers if way not in early]]
    sends = []
    for part in parts:
        starts = [held_cells + numbers[way] * half_slots for way in part]
        sends.append([c for start in starts for c in range(start, start + half_slots)])
    starts = [numbers[way] * half_slots for way in early]
    kept = [[c for c in range(start, start + half_slots)] for start in starts]
    sums, *others = sum_cells(cell, again, tens, coef, 2 * held_cells, sends + kept)
    local = {}
    for p, part in enumerate(parts):
        got = across(others[p])
        if p == 0:
            other_names = across(target * slots + slot_of)
            got, other_names, others[1] = apart((got, other_names, others[1]))
        if p == 1:
            got, tens_out = apart((got, tens))
            other_tens = across(tens_out)
        for k, way in enumerate(part):
            start = numbers[way] * half_slots
            mine = others[2 + k] if p == 0 else apart(sums[start : start + half_slots])
            other = apart(got[k * half_slots : (k + 1) * half_slots])
            local[way] = mine.astype(jnp.float32) + other.astype(jnp.float32)

    def add(value, held):
        return held if value is None else value.astype(jnp.float32) + held

    up, down, sent = [None, None], [None, None], ()
    for pair, step in turns:
        ahead, back = up[pair[0]], down[pair[1]]
        if ahead is not None:
            ahead, back, *sent = apart((ahead, back, *sent))
            if (pair, step) == turns[3]:
                ahead, names, other_names = apart((ahead, target * slots + slot_of, other_names))
        ahead = add(ahead, local[step, pair[0]]).astype(jnp.bfloat16)
        back = add(back, local[chips - step, pair[1]]).astype(jnp.bfloat16)
        sent = (ahead, back)
        up[pair[0]], down[pair[1]] = forward(ahead), backward(back)

    own = []
    for h in range(2):
        fitted = add(down[h], add(up[h], local[0, h])).astype(jnp.bfloat16)
        own.append(
            jnp.einsum(
                "sjp,pq->sjq", fitted, metric[0], preferred_element_type=jnp.float32
            ).astype(jnp.bfloat16)
        )

    tables = []
    for aux, slot in ((n // slots, n % slots) for n in (names, other_names)):
        held = jnp.where(aux % 2 == core, cell_of(aux, slot), held_cells)
        key = held * block_count + series
        rank = jnp.sum(jnp.where(key[None, :] < key[:, None], 1, 0), axis=1)
        order = jnp.sum(jnp.where(rank[None, :] == series[:, None], series[None, :], 0), axis=1)
        limits = jnp.arange(len(groups) + 1) * 2 * half_slots
        tables.append((jnp.sum(jnp.where(held[None, :] < limits[:, None], 1, 0), axis=1), order, held))
    tables = [jnp.stack(table) for table in zip(*tables)]

    both = (tens, other_tens)
    total = jnp.zeros((2, coef.shape[0], tens.shape[2]), jnp.float32)
    up, down = [forward(own[h]) for h in range(2)], [backward(own[h]) for h in range(2)]
    uses = [(pair, step) for step in range(1, far) for pair in (long, short)]
    total, *taken = apply_cells(len(groups) - 1, tables, total, both, own, 0 if uses else capacity)
    for pair, step in uses:
        ahead, back = up[pair[0]], down[pair[1]]
        ahead, back, total = apart((ahead, back, total))
        if step + 1 < far or pair == long:
            up[pair[0]], down[pair[1]] = forward(ahead), backward(back)
        group = groups.index([(chips - step, pair[0]), (step, pair[1])])
        takes = capacity if (pair, step) == uses[-1] else 0
        total, *more = apply_cells(group, tables, total, both, [ahead, back], takes)
        taken = more or taken
    (total,) = apply_cells(0, tables, total, taken, [up[0], down[1]], turned=True)
    return sum_over_cores_and_ctr(total, owners)


def slots_body(tens, coef, aux_of, slot_of, metric):
    owners = lax.axis_size("wide")
    block_count = tens.shape[0]
    capacity = max(2, 2 * block_count // owners)
    total_slots = owners * capacity
    half_form = jnp.einsum("jm,bpm->bjp", coef, tens, preferred_element_type=jnp.float32).astype(
        jnp.bfloat16
    )
    target = aux_of[:, 0]
    series = jnp.arange(block_count)
    matches = target[:, None] == target[None, :]
    earlier = series[None, :] < series[:, None]
    ranking = jnp.sum(jnp.where(matches & earlier, 1, 0), axis=1)
    position = target * capacity + ranking
    selector = position[None, :] == jnp.arange(total_slots)[:, None]
    selector_bf = jnp.where(selector, 1.0, 0.0).astype(jnp.bfloat16)
    outgoing = jnp.einsum(
        "kb,bjp->kjp", selector_bf, half_form, preferred_element_type=jnp.float32
    ).astype(jnp.bfloat16)
    slot_tags = jnp.sum(jnp.where(selector, slot_of[None, :] + 1, 0), axis=1)
    received, tags_in = (
        lax.all_to_all(outgoing, "wide", split_axis=0, concat_axis=0, tiled=True),
        lax.all_to_all(slot_tags, "wide", split_axis=0, concat_axis=0, tiled=True),
    )
    slot_onehot = jnp.where(
        tags_in[None, :] == (jnp.arange(OCC_DEV) + 1)[:, None], 1.0, 0.0
    ).astype(jnp.bfloat16)
    fitted = jnp.einsum(
        "sk,kjp->sjp", slot_onehot, received, preferred_element_type=jnp.float32
    ).astype(jnp.bfloat16)
    weighted = jnp.einsum(
        "sjp,pq->sjq", fitted, metric[0], preferred_element_type=jnp.float32
    ).astype(jnp.bfloat16)
    answers = jnp.einsum(
        "sk,sjq->kjq", slot_onehot, weighted, preferred_element_type=jnp.float32
    ).astype(jnp.bfloat16)
    returned = lax.all_to_all(answers, "wide", split_axis=0, concat_axis=0, tiled=True)
    per_block = jnp.einsum(
        "kb,kjq->bjq", selector_bf, returned, preferred_element_type=jnp.float32
    ).astype(jnp.bfloat16)
    partial_value = jnp.einsum("bjq,bqm->jm", per_block, tens, preferred_element_type=jnp.float32)
    return sum_over_ctr(partial_value)


def body(tens, coef, aux_of, slot_of, metric):
    owners, block_count = lax.axis_size("wide"), tens.shape[0]
    dense = owners * OCC_DEV <= 2 * block_count and owners % 4 == 0 and block_count % 64 == 0
    return (cells_body if dense else slots_body)(tens, coef, aux_of, slot_of, metric)


def solution(mesh):
    placed = (
        P(("wide", "ctr"), None, None),
        P(None, "wide"),
        P(("wide", "ctr"), None),
        P(("wide", "ctr")),
        P("wide", None, None),
    )
    return jax.shard_map(
        body, mesh=mesh, in_specs=placed, out_specs=P(None, ("wide", "ctr")), check_vma=False
    )
```
